512 devices in a mesh: group: 32 (over y, x), section: 16 (over z, core).
Axes of the slice: x: 4, y: 8, z: 8, core: 2. Of those that a mesh axis runs over, the one named last changes fastest.
Arguments:
- columns: float32 [32, 32, 16, 8192], P('group', None, None, 'section'), may hold values from -6 to 6
- vectors: bfloat16 [32, 8, 128, 8192], P('group', None, None, 'section'), may hold values from -0.0625 to 0.0625
- factors: float32 [32, 8, 128, 128], P('group'), as said below
- order: int32 [32], P('group'), may hold values from 4096 to 8192
- blocks: int32 [32], P('group'), may hold values from 1 to 8
- live: int32 [32, 32], P('group'), may hold values from 0 to 16
Outputs:
- result: float32 [32, 32, 16, 8192], P('group', None, None, 'section')
The draws below stay inside these ranges and needn't reach their ends.
Inputs may be any that keep to these rules, and one draw needn't show every extreme that they name: `factors`: upper triangular, diagonal entries between one half and two, off-diagonal entries small.
All inputs are finite; a program needn't handle non-finite values.
Results may differ from the reference program's by a relative error of at most 0.0003.
Values sent between devices are 32-bit elements; how exact they have to be, the bound alone decides.
A program may use at most 64 MiB of HBM per device.

```python
import jax
import jax.numpy as jnp
from jax import lax

N = 8192
BW = 128
NB = 8
SLOTS = 16
GROUPS = 32


def draw_factors(key, part):
    first, second = jax.random.split(jax.random.fold_in(key, 17))
    shape = (GROUPS, NB, BW, BW)
    diag = jax.random.uniform(first, shape[:3], jnp.float32, 0.5, 1.5)
    upper = 0.03 * jax.random.normal(second, shape, jnp.float32)
    strict = jnp.triu(jnp.ones((BW, BW), jnp.float32), 1)
    return upper * strict + diag[..., None] * jnp.eye(BW, dtype=jnp.float32)


def touch_ends(result, key, low, top_value):
    spot = [jax.random.randint(jax.random.fold_in(key, axis), (), 0, length) for axis, length in enumerate(result.shape)]
    longest = result.shape.index(max(result.shape))
    next_to = spot[:longest] + [(spot[longest] + 1) % result.shape[longest]] + spot[longest + 1:]
    return result.at[tuple(spot)].set(low).at[tuple(next_to)].set(top_value)


def level_of(own_key, shape, cuts, low, largest):
    level, own = 1.0, jax.random.fold_in(own_key, 6)
    for dim, shards_of in cuts:
        steps = jnp.exp(jax.random.uniform(jax.random.fold_in(own, dim), (shards_of,), jnp.float32, low / len(cuts), largest / len(cuts)))
        level = level * jnp.repeat(steps, shape[dim] // shards_of).reshape([-1 if axis == dim else 1 for axis in range(len(shape))])
    return level


def centred(rng, dims, spread, limit, pieces=(), kind=jnp.bfloat16):
    loudness = level_of(rng, dims, pieces, -0.22, 0.18) if pieces else 1.0
    values = jax.random.normal(rng, dims, jnp.float32) * spread * loudness
    return jnp.minimum(jnp.maximum(values, -limit), limit).astype(kind)


def setup_inputs(seed: int = 0) -> dict:
    key_list = jax.random.split(jax.random.key(seed), 7)
    return {
        "columns": centred(key_list[0], (GROUPS, GROUPS, SLOTS, N), 1.0, 6.0, ((0, 32), (3, 16)), jnp.float32),
        "vectors": centred(key_list[1], (GROUPS, NB, BW, N), N ** -0.5, 0.0625, ((0, 32), (3, 16))),
        "factors": draw_factors(jax.random.fold_in(key_list[6], 71), 0),
        "order": touch_ends(jax.random.randint(key_list[3], (GROUPS,), N // 2, N + 1), jax.random.fold_in(key_list[3], 1), N // 2, N).astype(jnp.int32),
        "blocks": touch_ends(jax.random.randint(key_list[4], (GROUPS,), 1, NB + 1), jax.random.fold_in(key_list[4], 1), 1, NB).astype(jnp.int32),
        "live": touch_ends(jax.random.randint(key_list[5], (GROUPS, GROUPS), 0, SLOTS + 1), jax.random.fold_in(key_list[5], 1), 0, SLOTS).astype(jnp.int32),
    }


def transform(panel, vectors_g, factors_g, size, count):
    inside = (jnp.arange(N) < size).astype(jnp.float32)
    for index in reversed(range(NB)):
        basis = vectors_g[index].astype(jnp.float32) * inside[None, :]
        active = (index < count).astype(jnp.float32)
        factor = factors_g[index] * active
        inner = jnp.dot(panel, basis.T, precision=lax.Precision.HIGHEST)
        scaled = jnp.dot(inner, factor.T, precision=lax.Precision.HIGHEST)
        panel = panel - jnp.dot(scaled, basis, precision=lax.Precision.HIGHEST)
    return panel


def reference(columns, vectors, factors, order, blocks, live):
    def one_matrix(home):
        panel = columns[:, home].reshape(GROUPS * SLOTS, N)
        panel = transform(panel, vectors[home], factors[home], order[home], blocks[home])
        return panel.reshape(GROUPS, SLOTS, N)

    outcome = lax.map(one_matrix, jnp.arange(GROUPS, dtype=jnp.int32))
    outcome = jnp.transpose(outcome, (1, 0, 2, 3))
    keep = jnp.arange(SLOTS, dtype=jnp.int32)[None, None, :] < live[:, :, None]
    return jnp.where(keep[..., None], outcome, jnp.float32(0.0)).astype(jnp.float32)
```

```python
import functools

import jax
import jax.numpy as jnp
from jax import lax
from jax.experimental import pallas as pl
from jax.experimental.pallas import tpu as pltpu
from jax.sharding import PartitionSpec as P

MESH = pl.DeviceIdType.MESH
F32 = jnp.float32
BF16 = jnp.bfloat16
HIGH = lax.Precision.HIGHEST
STREAMS = 2


def three(x):
    first = x.astype(BF16)
    rest = x - first.astype(F32)
    second = rest.astype(BF16)
    third = (rest - second.astype(F32)).astype(BF16)
    return first, second, third


def times(a, b):
    return jnp.dot(a, b, preferred_element_type=F32)


def exact(a, b):
    return jnp.dot(a, b, precision=HIGH, preferred_element_type=F32)


def against(a, b):
    return lax.dot_general(a, b, (((1,), (1,)), ((), ())), preferred_element_type=F32)


class Place:
    def __init__(self, ring):
        self.ring = ring
        self.long = ring // 2
        self.short = ring - 1 - self.long
        self.group = lax.axis_index("group")
        self.section = lax.axis_index("section")
        self.z = self.section // 2
        self.core = lax.rem(self.section, 2)
        self.way = 1 - 2 * self.core

    def at(self, steps):
        return lax.rem(self.z + self.way * steps + 2 * self.ring, self.ring)

    def neighbour(self, steps):
        return (self.group, self.at(steps) * 2 + self.core)

    def partner(self):
        return (self.group, self.z * 2 + 1 - self.core)


class Sum:
    def __init__(self, place, src, swapped, far, near, full, sent, swap_sem, ring_sem, gather_sem):
        self.p = place
        self.src, self.swapped, self.far, self.near, self.full = src, swapped, far, near, full
        self.sent, self.swap_sem, self.ring_sem, self.gather_sem = sent, swap_sem, ring_sem, gather_sem
        self.rows = far.shape[1]

    def piece(self, ref, z, core):
        start = pl.multiple_of((z * 2 + core) * self.rows, self.rows)
        return ref.at[pl.ds(start, self.rows)]

    def send(self, src, dst, which, recv, device):
        return pltpu.make_async_remote_copy(
            src_ref=src,
            dst_ref=dst,
            send_sem=self.sent.at[which],
            recv_sem=recv,
            device_id=device,
            device_id_type=MESH,
        )

    def arrived(self, dst, recv):
        self.send(dst, dst, 0, recv, self.p.partner()).wait_recv()

    def swap(self):
        p = self.p
        steps = []
        for t in range(p.long):
            steps.append(p.long - t)
            if t < p.short:
                steps.append(t - p.short)
        for k in steps + [0]:
            z = p.at(-k)
            self.send(
                self.piece(self.src, z, 1 - p.core), self.swapped.at[z], 0, self.swap_sem.at[0, z], p.partner()
            ).start()

    def own(self, z):
        self.arrived(self.swapped.at[z], self.swap_sem.at[0, z])
        return self.piece(self.src, z, self.p.core)[...] + self.swapped[z]

    def hop(self, buffers, sem, t, z, device):
        mine = self.own(z)
        if t == 0:
            self.swapped[z] = mine
            source = self.swapped.at[z]
        else:
            self.arrived(buffers.at[t - 1], self.ring_sem.at[sem, t - 1])
            buffers[t - 1] = buffers[t - 1] + mine
            source = buffers.at[t - 1]
        self.send(source, buffers.at[t], 0, self.ring_sem.at[sem, t], device).start()

    def step(self, t):
        p = self.p
        self.hop(self.far, 0, t, p.at(p.long - t), p.neighbour(1))
        if t < p.short:
            self.hop(self.near, 1, t, p.at(t - p.short), p.neighbour(-1))

    def total(self):
        p = self.p
        mine = self.own(p.z)
        self.arrived(self.far.at[p.long - 1], self.ring_sem.at[0, p.long - 1])
        self.arrived(self.near.at[p.short - 1], self.ring_sem.at[1, p.short - 1])
        return mine + self.far[p.long - 1] + self.near[p.short - 1]

    def forward(self, origin, t):
        p = self.p
        piece = self.piece(self.full, origin, p.core)
        if t >= 0 and t < p.long:
            self.send(piece, piece, 1, self.gather_sem.at[0, t], p.neighbour(1)).start()
        if t <= 0 and -t < p.short:
            self.send(piece, piece, 1, self.gather_sem.at[1, -t], p.neighbour(-1)).start()
        self.send(piece, piece, 1, self.swap_sem.at[1, origin], p.partner()).start()

    def spread(self, value):
        p = self.p
        self.piece(self.full, p.z, p.core)[...] = value
        self.forward(p.z, 0)

    def relay(self, t):
        p = self.p
        origin = p.at(-t)
        self.arrived(self.piece(self.full, origin, p.core), self.gather_sem.at[0, t - 1])
        self.forward(origin, t)
        if t <= p.short:
            origin = p.at(t)
            self.arrived(self.piece(self.full, origin, p.core), self.gather_sem.at[1, t - 1])
            self.forward(origin, -t)

    def gathered(self):
        p = self.p
        for z in range(p.ring):
            self.arrived(self.piece(self.full, z, 1 - p.core), self.swap_sem.at[1, z])

    def drain(self):
        pieces = 2 * self.p.ring - 1
        whole = self.full.at[pl.ds(0, pieces * self.rows)]
        for which in range(2):
            self.send(whole, whole, which, self.swap_sem.at[0, 0], self.p.partner()).wait_send()


def kernel(
    groups,
    ring,
    columns,
    vectors,
    factors,
    order,
    blocks,
    out,
    raw,
    facts,
    basis,
    panel,
    moved,
    g_src,
    g_swapped,
    g_far,
    g_near,
    g_full,
    tri,
    tri_parts,
    w_src,
    w_swapped,
    w_far,
    w_near,
    w_full,
    load_sem,
    in_send,
    in_recv,
    out_send,
    out_recv,
    sent,
    swap_sem,
    ring_sem,
    gather_sem,
):
    p = Place(ring)
    me, section = p.group, p.section
    count, width, rows = raw.shape
    slots = panel.shape[1] // groups

    barrier = pltpu.get_barrier_semaphore()

    def greet(d, carry):
        peer = lax.rem(me + d, groups)
        pl.semaphore_signal(barrier, inc=1, device_id=(peer, section), device_id_type=MESH)
        return carry

    lax.fori_loop(1, groups, greet, 0)
    for other in (p.neighbour(1), p.neighbour(-1), p.partner()):
        pl.semaphore_signal(barrier, inc=1, device_id=other, device_id_type=MESH)

    loads = [
        pltpu.make_async_copy(vectors.at[0], raw, load_sem.at[0]),
        pltpu.make_async_copy(factors.at[0], facts, load_sem.at[1]),
    ]
    for s in range(STREAMS):
        loads.append(
            pltpu.make_async_copy(
                columns.at[0, me, pl.ds(s * slots, slots)],
                panel.at[s, pl.ds(pl.multiple_of(me * slots, slots), slots)],
                load_sem.at[2 + s],
            )
        )
    for load in loads:
        load.start()
    tri[...] = jnp.zeros_like(tri)
    loads[0].wait()
    row = section * rows + lax.broadcasted_iota(jnp.int32, (width, rows), 1)
    inside = row < order[0]
    for j in range(count):
        block = jnp.where(inside, raw[j].astype(F32), 0.0)
        basis[pl.ds(j * width, width)] = block.astype(BF16)

    pl.semaphore_wait(barrier, groups + 2)

    def exchange(s, source, target, send_sem, recv_sem):
        def one(k, carry):
            half = (k + 1) // 2
            d = groups // 2 + (2 * lax.rem(k, 2) - 1) * half
            peer = lax.rem(me + d, groups)
            pltpu.make_async_remote_copy(
                src_ref=source(peer),
                dst_ref=target(me),
                send_sem=send_sem,
                recv_sem=recv_sem,
                device_id=(peer, section),
                device_id_type=MESH,
            ).start()
            return carry

        lax.fori_loop(0, groups - 1, one, 0)

    def lines(ref, s):
        return lambda g: ref.at[s, pl.ds(pl.multiple_of(g * slots, slots), slots)]

    def slab(ref, s):
        return lambda g: ref.at[0, g, pl.ds(s * slots, slots)]

    for s in range(STREAMS):
        exchange(s, slab(columns, s), lines(panel, s), in_send.at[s], in_recv.at[s])

    place_of = {}
    for k in range(1, count):
        low = against(basis[pl.ds(k * width, width)], basis[pl.ds(0, k * width)])
        for j in range(k):
            place_of[k, j] = len(place_of)
            g_src[pl.ds(place_of[k, j] * width, width)] = low[:, j * width : (j + 1) * width]

    gram = Sum(p, g_src, g_swapped, g_far, g_near, g_full, sent.at[0], swap_sem.at[0], ring_sem.at[0], gather_sem.at[0])
    parts = [
        Sum(
            p,
            w_src.at[s],
            w_swapped.at[s],
            w_far.at[s],
            w_near.at[s],
            w_full.at[s],
            sent.at[1 + s],
            swap_sem.at[1 + s],
            ring_sem.at[1 + s],
            gather_sem.at[1 + s],
        )
        for s in range(STREAMS)
    ]
    gram.swap()
    loads[1].wait()
    for j in range(count):
        factor = jnp.where(j < blocks[0], facts[j], 0.0)
        tri[pl.ds(j * width, width), pl.ds(j * width, width)] = factor.T
    for t in range(p.long):
        gram.step(t)
    gram.spread(gram.total())
    for t in range(1, p.long + 1):
        gram.relay(t)
    gram.gathered()

    def low_block(first, size):
        lines = []
        for k in range(first + size, first + 2 * size):
            lines.append(
                jnp.concatenate(
                    [g_full[pl.ds(place_of[k, j] * width, width)] for j in range(first, first + size)], axis=1
                )
            )
        return jnp.concatenate(lines, axis=0)

    def merge(first, size):
        top = pl.ds(first * width, size * width)
        low = pl.ds((first + size) * width, size * width)
        tri[low, top] = -exact(tri[low, low], exact(low_block(first, size), tri[top, top]))

    def split():
        for i, part in enumerate(three(tri[...])):
            tri_parts[i] = part

    def peer_lines(s):
        whole = panel.at[s, pl.ds(0, (groups - 1) * slots)]
        return whole

    def bring(s):
        loads[2 + s].wait()
        whole = peer_lines(s)
        pltpu.make_async_remote_copy(
            whole, whole, in_send.at[s], in_recv.at[s], device_id=p.partner(), device_id_type=MESH
        ).wait_recv()
        a, b, c = three(panel[s])
        v = basis[...]
        w_src[s] = against(c, v) + against(b, v) + against(a, v)

    def scaled(total):
        a, b, c = three(total)
        half = tri.shape[0] // 2
        done = []
        for first, last, start in ((0, half, 0), (half, 2 * half, half)):
            t0, t1, t2 = (tri_parts[i, start:, first:last] for i in range(3))
            a_, b_, c_ = a[:, start:], b[:, start:], c[:, start:]
            small = times(c_, t0) + times(b_, t1) + times(a_, t2)
            done.append(small + times(b_, t0) + times(a_, t1) + times(a_, t0))
        return jnp.concatenate(done, axis=1)

    def leave(s):
        a, b, c = three(w_full[s])
        v = basis[...]
        moved[s] = panel[s] - (times(c, v) + times(b, v) + times(a, v))
        exchange(s, lines(moved, s), slab(out, s), out_send.at[s], out_recv.at[s])
        own = pltpu.make_async_copy(lines(moved, s)(me), slab(out, s)(me), load_sem.at[2 + s])
        own.start()
        return own

    bring(0)
    parts[0].swap()
    for first in range(0, count, 2):
        merge(first, 1)
    parts[0].step(0)
    for first in range(0, count, 4):
        merge(first, 2)
    parts[0].step(1)
    merge(0, count // 2)
    for t in range(2, p.long):
        parts[0].step(t)
    split()
    bring(1)
    parts[1].swap()
    parts[0].spread(scaled(parts[0].total()))
    for t in range(p.long):
        parts[1].step(t)
        parts[0].relay(t + 1)
    parts[1].spread(scaled(parts[1].total()))
    parts[0].gathered()
    own0 = leave(0)
    for t in range(p.long):
        parts[1].relay(t + 1)
    parts[1].gathered()
    own1 = leave(1)

    gram.drain()
    for s in range(STREAMS):
        parts[s].drain()
    own0.wait()
    own1.wait()
    for s in range(STREAMS):
        whole = peer_lines(s)
        pltpu.make_async_remote_copy(
            whole, whole, in_send.at[s], in_recv.at[s], device_id=p.partner(), device_id_type=MESH
        ).wait_send()
        there = pltpu.make_async_remote_copy(
            whole, whole, out_send.at[s], out_recv.at[s], device_id=p.partner(), device_id_type=MESH
        )
        there.wait_send()
        there.wait_recv()


def shards(groups, ring, columns, vectors, factors, order, blocks, live):
    _, count, width, rows = vectors.shape
    slots = columns.shape[2]
    each = slots // STREAMS
    lines = groups * each
    merged = count * width
    long, short = ring // 2, ring - 1 - ring // 2
    gram = count * (count - 1) // 2 * width
    g_piece, w_piece = gram // (2 * ring), lines // (2 * ring)
    anywhere = pl.BlockSpec(memory_space=pl.ANY)
    scalars = pl.BlockSpec(memory_space=pltpu.SMEM)
    returned = pl.pallas_call(
        functools.partial(kernel, groups, ring),
        out_shape=jax.ShapeDtypeStruct(columns.shape, F32),
        in_specs=[anywhere, anywhere, anywhere, scalars, scalars],
        out_specs=anywhere,
        scratch_shapes=[
            pltpu.VMEM((count, width, rows), BF16),
            pltpu.VMEM((count, width, width), F32),
            pltpu.VMEM((merged, rows), BF16),
            pltpu.VMEM((STREAMS, lines, rows), F32),
            pltpu.VMEM((STREAMS, lines, rows), F32),
            pltpu.VMEM((gram, width), F32),
            pltpu.VMEM((ring, g_piece, width), F32),
            pltpu.VMEM((long, g_piece, width), F32),
            pltpu.VMEM((short, g_piece, width), F32),
            pltpu.VMEM((gram, width), F32),
            pltpu.VMEM((merged, merged), F32),
            pltpu.VMEM((3, merged, merged), BF16),
            pltpu.VMEM((STREAMS, lines, merged), F32),
            pltpu.VMEM((STREAMS, ring, w_piece, merged), F32),
            pltpu.VMEM((STREAMS, long, w_piece, merged), F32),
            pltpu.VMEM((STREAMS, short, w_piece, merged), F32),
            pltpu.VMEM((STREAMS, lines, merged), F32),
            pltpu.SemaphoreType.DMA((2 + STREAMS,)),
            pltpu.SemaphoreType.DMA((STREAMS,)),
            pltpu.SemaphoreType.DMA((STREAMS,)),
            pltpu.SemaphoreType.DMA((STREAMS,)),
            pltpu.SemaphoreType.DMA((STREAMS,)),
            pltpu.SemaphoreType.DMA((1 + STREAMS, 2)),
            pltpu.SemaphoreType.DMA((1 + STREAMS, 2, ring)),
            pltpu.SemaphoreType.DMA((1 + STREAMS, 2, long)),
            pltpu.SemaphoreType.DMA((1 + STREAMS, 2, long)),
        ],
        compiler_params=pltpu.CompilerParams(
            collective_id=0, has_side_effects=True, vmem_limit_bytes=60 * 1024 * 1024
        ),
        name="back_transform",
    )(columns, vectors, factors, order, blocks)
    keep = jnp.arange(slots)[None, :] < live[0][:, None]
    return jnp.where(keep[None, :, :, None], returned, jnp.float32(0.0))


def solution(mesh):
    groups, ring = mesh.shape["group"], mesh.shape["section"] // 2
    placed = (
        P("group", None, None, "section"),
        P("group", None, None, "section"),
        P("group", None, None, None),
        P("group"),
        P("group"),
        P("group", None),
    )
    return jax.shard_map(
        functools.partial(shards, groups, ring),
        mesh=mesh,
        in_specs=placed,
        out_specs=P("group", None, None, "section"),
        check_vma=False,
    )
```

```python
import functools

import jax
import jax.numpy as jnp
from jax import lax
from jax.experimental import pallas as pl
from jax.experimental.pallas import tpu as pltpu
from jax.sharding import PartitionSpec as P

MESH = pl.DeviceIdType.MESH
F32 = jnp.float32
BF16 = jnp.bfloat16
STREAMS = 2
GRAM_CUTS = 4
PART_CUTS = 2


def halves(x):
    first = x.astype(BF16)
    return first, (x - first.astype(F32)).astype(BF16)


def times(a, b):
    return jnp.dot(a, b, preferred_element_type=F32)


def product(a, b):
    return times(a[1], b[0]) + times(a[0], b[1]) + times(a[0], b[0])


def against(a, b):
    return lax.dot_general(a, b, (((1,), (1,)), ((), ())), preferred_element_type=F32)


def tree(ring):
    long = ring // 2
    up = {k: k - 1 for k in range(1, long + 1)}
    up.update({-k: 1 - k for k in range(1, ring - long)})
    if long == 4:
        up[3] = 1
    levels, left = [], set(up)
    while left:
        now = [k for k in left if not any(up[c] == k for c in left)]
        levels.append(sorted(now, key=lambda k: -abs(k)))
        left -= set(now)
    return levels, up


class Place:
    def __init__(self, ring):
        self.ring = ring
        self.levels, self.up = tree(ring)
        self.edges = sorted(self.up)
        strides = {k - self.up[k] for k in self.edges}
        self.near = sorted(strides | {-stride for stride in strides})
        self.group = lax.axis_index("group")
        self.section = lax.axis_index("section")
        self.z = self.section // 2
        self.core = lax.rem(self.section, 2)
        self.way = 1 - 2 * self.core

    def at(self, steps):
        return lax.rem(self.z + self.way * steps + 2 * self.ring, self.ring)

    def neighbour(self, steps):
        return (self.group, self.at(steps) * 2 + self.core)

    def partner(self):
        return (self.group, self.z * 2 + 1 - self.core)


class Sum:
    def __init__(self, place, cuts, src, swapped, landed, full, sent, swap_sem, ring_sem, gather_sem):
        self.p, self.cuts = place, cuts
        self.src, self.swapped, self.landed, self.full = src, swapped, landed, full
        self.sent, self.swap_sem, self.ring_sem, self.gather_sem = sent, swap_sem, ring_sem, gather_sem
        self.rows = landed.shape[1]
        self.part = self.rows // cuts

    def piece(self, ref, z, core, cut=None):
        start = pl.multiple_of((z * 2 + core) * self.rows, self.part)
        if cut is None:
            return ref.at[pl.ds(start, self.rows)]
        return ref.at[pl.ds(pl.multiple_of(start + cut * self.part, self.part), self.part)]

    def some(self, ref, at, cut):
        return ref.at[at, pl.ds(cut * self.part, self.part)]

    def send(self, src, dst, which, recv, device):
        return pltpu.make_async_remote_copy(
            src_ref=src,
            dst_ref=dst,
            send_sem=self.sent.at[which],
            recv_sem=recv,
            device_id=device,
            device_id_type=MESH,
        )

    def arrived(self, dst, recv):
        self.send(dst, dst, 0, recv, self.p.partner()).wait_recv()

    def swap(self):
        p = self.p
        for k in [k for level in p.levels for k in level] + [0]:
            z = p.at(-k)
            self.send(
                self.piece(self.src, z, 1 - p.core), self.swapped.at[z], 0, self.swap_sem.at[0, z], p.partner()
            ).start()

    def own(self, z, cut):
        return self.piece(self.src, z, self.p.core, cut)[...] + self.some(self.swapped, z, cut)[...]

    def gain(self, k, z, cut):
        value = self.own(z, cut)
        for e, below in enumerate(self.p.edges):
            if self.p.up[below] == k:
                part = self.some(self.landed, e, cut)
                self.arrived(part, self.ring_sem.at[e, cut])
                value = value + part[...]
        return value

    def step(self, level):
        p = self.p
        for k in p.levels[level]:
            z = p.at(k)
            self.arrived(self.swapped.at[z], self.swap_sem.at[0, z])
        for cut in range(self.cuts):
            for k in p.levels[level]:
                z, e = p.at(k), p.edges.index(k)
                source = self.some(self.swapped, z, cut)
                source[...] = self.gain(k, z, cut)
                self.send(
                    source, self.some(self.landed, e, cut), 0, self.ring_sem.at[e, cut], p.neighbour(k - p.up[k])
                ).start()

    def total(self, cut):
        p = self.p
        if cut == 0:
            self.arrived(self.swapped.at[p.z], self.swap_sem.at[0, p.z])
        return self.gain(0, p.z, cut)

    def forward(self, k, cut):
        p = self.p
        origin = p.at(-k)
        part = self.piece(self.full, origin, p.core, cut)
        if k:
            self.arrived(part, self.gather_sem.at[p.edges.index(k), cut])
        for e, beyond in sorted(enumerate(p.edges), key=lambda pair: -abs(pair[1])):
            if p.up[beyond] == k:
                self.send(part, part, 1, self.gather_sem.at[e, cut], p.neighbour(beyond - k)).start()
        self.send(part, part, 1, self.swap_sem.at[1, origin], p.partner()).start()

    def spread(self, value, cut):
        p = self.p
        self.piece(self.full, p.z, p.core, cut)[...] = value
        self.forward(0, cut)

    def relay(self, level):
        for cut in range(self.cuts):
            for k in self.p.levels[len(self.p.levels) - level]:
                self.forward(k, cut)

    def gathered(self):
        p = self.p
        for z in range(p.ring):
            self.arrived(self.piece(self.full, z, 1 - p.core), self.swap_sem.at[1, z])

    def drain(self):
        pieces = 2 * self.p.ring - 1
        whole = self.full.at[pl.ds(0, pieces * self.rows)]
        for which in range(2):
            self.send(whole, whole, which, self.swap_sem.at[0, 0], self.p.partner()).wait_send()


def kernel(
    groups,
    ring,
    columns,
    vectors,
    factors,
    order,
    blocks,
    out,
    raw,
    facts,
    basis,
    panel,
    moved,
    g_src,
    g_swapped,
    g_landed,
    g_full,
    turned,
    scaled,
    w_src,
    w_swapped,
    w_landed,
    w_full,
    load_sem,
    in_send,
    in_recv,
    out_send,
    out_recv,
    sent,
    swap_sem,
    gram_ring,
    gram_gather,
    ring_sem,
    gather_sem,
):
    p = Place(ring)
    me, section = p.group, p.section
    count, width, rows = raw.shape
    slots = panel.shape[1] // groups

    barrier = pltpu.get_barrier_semaphore()

    def greet(d, carry):
        peer = lax.rem(me + d, groups)
        pl.semaphore_signal(barrier, inc=1, device_id=(peer, section), device_id_type=MESH)
        return carry

    lax.fori_loop(1, groups, greet, 0)
    for other in [p.neighbour(stride) for stride in p.near] + [p.partner()]:
        pl.semaphore_signal(barrier, inc=1, device_id=other, device_id_type=MESH)

    loads = [
        pltpu.make_async_copy(vectors.at[0], raw, load_sem.at[0]),
        pltpu.make_async_copy(factors.at[0], facts, load_sem.at[1]),
    ]
    for s in range(STREAMS):
        loads.append(
            pltpu.make_async_copy(
                columns.at[0, me, pl.ds(s * slots, slots)],
                panel.at[s, pl.ds(pl.multiple_of(me * slots, slots), slots)],
                load_sem.at[2 + s],
            )
        )
    for load in loads:
        load.start()
    loads[0].wait()
    row = section * rows + lax.broadcasted_iota(jnp.int32, (width, rows), 1)
    inside = row < order[0]
    for j in range(count):
        block = jnp.where(inside, raw[j].astype(F32), 0.0)
        basis[pl.ds(j * width, width)] = block.astype(BF16)

    def exchange(s, source, target, send_sem, recv_sem):
        def one(k, carry):
            half = (k + 1) // 2
            d = groups // 2 + (2 * lax.rem(k, 2) - 1) * half
            peer = lax.rem(me + d, groups)
            pltpu.make_async_remote_copy(
                src_ref=source(peer),
                dst_ref=target(me),
                send_sem=send_sem,
                recv_sem=recv_sem,
                device_id=(peer, section),
                device_id_type=MESH,
            ).start()
            return carry

        lax.fori_loop(0, groups - 1, one, 0)

    def lines(ref, s):
        return lambda g: ref.at[s, pl.ds(pl.multiple_of(g * slots, slots), slots)]

    def slab(ref, s):
        return lambda g: ref.at[0, g, pl.ds(s * slots, slots)]

    place_of = {}
    for k in range(1, count):
        low = against(basis[pl.ds(k * width, width)], basis[pl.ds(0, k * width)])
        for j in range(k):
            place_of[k, j] = len(place_of)
            g_src[pl.ds(place_of[k, j] * width, width)] = low[:, j * width : (j + 1) * width]

    gram = Sum(
        p, GRAM_CUTS, g_src, g_swapped, g_landed, g_full, sent.at[0], swap_sem.at[0], gram_ring, gram_gather
    )
    parts = [
        Sum(
            p,
            PART_CUTS,
            w_src.at[s],
            w_swapped.at[s],
            w_landed.at[s],
            w_full.at[s],
            sent.at[1 + s],
            swap_sem.at[1 + s],
            ring_sem.at[s],
            gather_sem.at[s],
        )
        for s in range(STREAMS)
    ]
    pl.semaphore_wait(barrier, groups + len(p.near))
    gram.swap()
    exchange(0, slab(columns, 0), lines(panel, 0), in_send.at[0], in_recv.at[0])
    gram.step(0)
    for s in range(1, STREAMS):
        exchange(s, slab(columns, s), lines(panel, s), in_send.at[s], in_recv.at[s])
    loads[1].wait()
    for j in range(count):
        factor = jnp.where(j < blocks[0], facts[j], 0.0)
        turned[j] = factor.T
    gram.step(1)
    gram.step(2)
    def substitute(j):
        here, before = pl.ds(j * width, width), pl.ds(0, j * width)
        value = basis[here].astype(F32)
        if j:
            crossed = [g_full[pl.ds(place_of[j, i] * width, width)] for i in range(j)]
            crossed = halves(jnp.concatenate(crossed, axis=1))
            value = value - product(crossed, (scaled[0, before], scaled[1, before]))
        for i, part in enumerate(halves(product(halves(turned[j]), halves(value)))):
            scaled[i, here] = part

    def peer_lines(s):
        whole = panel.at[s, pl.ds(0, (groups - 1) * slots)]
        return whole

    def bring(s):
        loads[2 + s].wait()
        whole = peer_lines(s)
        pltpu.make_async_remote_copy(
            whole, whole, in_send.at[s], in_recv.at[s], device_id=p.partner(), device_id_type=MESH
        ).wait_recv()
        a, b = halves(panel[s])
        v = basis[...]
        w_src[s] = against(b, v) + against(a, v)

    def leave(s):
        moved[s] = panel[s] - product(halves(w_full[s]), (scaled[0], scaled[1]))
        exchange(s, lines(moved, s), slab(out, s), out_send.at[s], out_recv.at[s])
        own = pltpu.make_async_copy(lines(moved, s)(me), slab(out, s)(me), load_sem.at[2 + s])
        own.start()
        return own

    def finish(s):
        for cut in range(PART_CUTS):
            parts[s].spread(parts[s].total(cut), cut)

    bring(0)
    parts[0].swap()
    for cut in range(GRAM_CUTS):
        gram.spread(gram.total(cut), cut)
    parts[0].step(0)
    gram.relay(1)
    parts[0].step(1)
    gram.relay(2)
    parts[0].step(2)
    bring(1)
    parts[1].swap()
    gram.relay(3)
    finish(0)
    parts[1].step(0)
    gram.gathered()
    for j in range(0, 3):
        substitute(j)
    parts[0].relay(1)
    parts[1].step(1)
    for j in range(3, 6):
        substitute(j)
    parts[0].relay(2)
    parts[1].step(2)
    for j in range(6, count):
        substitute(j)
    parts[0].relay(3)
    finish(1)
    parts[0].gathered()
    own0 = leave(0)
    parts[1].relay(1)
    parts[1].relay(2)
    parts[1].relay(3)
    parts[1].gathered()
    own1 = leave(1)

    gram.drain()
    for s in range(STREAMS):
        parts[s].drain()
    own0.wait()
    own1.wait()
    for s in range(STREAMS):
        whole = peer_lines(s)
        pltpu.make_async_remote_copy(
            whole, whole, in_send.at[s], in_recv.at[s], device_id=p.partner(), device_id_type=MESH
        ).wait_send()
        there = pltpu.make_async_remote_copy(
            whole, whole, out_send.at[s], out_recv.at[s], device_id=p.partner(), device_id_type=MESH
        )
        there.wait_send()
        there.wait_recv()


def shards(groups, ring, columns, vectors, factors, order, blocks, live):
    _, count, width, rows = vectors.shape
    slots = columns.shape[2]
    each = slots // STREAMS
    lines = groups * each
    merged = count * width
    gram = count * (count - 1) // 2 * width
    g_piece, w_piece = gram // (2 * ring), lines // (2 * ring)
    anywhere = pl.BlockSpec(memory_space=pl.ANY)
    scalars = pl.BlockSpec(memory_space=pltpu.SMEM)
    returned = pl.pallas_call(
        functools.partial(kernel, groups, ring),
        out_shape=jax.ShapeDtypeStruct(columns.shape, F32),
        in_specs=[anywhere, anywhere, anywhere, scalars, scalars],
        out_specs=anywhere,
        scratch_shapes=[
            pltpu.VMEM((count, width, rows), BF16),
            pltpu.VMEM((count, width, width), F32),
            pltpu.VMEM((merged, rows), BF16),
            pltpu.VMEM((STREAMS, lines, rows), F32),
            pltpu.VMEM((STREAMS, lines, rows), F32),
            pltpu.VMEM((gram, width), F32),
            pltpu.VMEM((ring, g_piece, width), F32),
            pltpu.VMEM((ring - 1, g_piece, width), F32),
            pltpu.VMEM((gram, width), F32),
            pltpu.VMEM((count, width, width), F32),
            pltpu.VMEM((2, merged, rows), BF16),
            pltpu.VMEM((STREAMS, lines, merged), F32),
            pltpu.VMEM((STREAMS, ring, w_piece, merged), F32),
            pltpu.VMEM((STREAMS, ring - 1, w_piece, merged), F32),
            pltpu.VMEM((STREAMS, lines, merged), F32),
            pltpu.SemaphoreType.DMA((2 + STREAMS,)),
            pltpu.SemaphoreType.DMA((STREAMS,)),
            pltpu.SemaphoreType.DMA((STREAMS,)),
            pltpu.SemaphoreType.DMA((STREAMS,)),
            pltpu.SemaphoreType.DMA((STREAMS,)),
            pltpu.SemaphoreType.DMA((1 + STREAMS, 2)),
            pltpu.SemaphoreType.DMA((1 + STREAMS, 2, ring)),
            pltpu.SemaphoreType.DMA((ring - 1, GRAM_CUTS)),
            pltpu.SemaphoreType.DMA((ring - 1, GRAM_CUTS)),
            pltpu.SemaphoreType.DMA((STREAMS, ring - 1, PART_CUTS)),
            pltpu.SemaphoreType.DMA((STREAMS, ring - 1, PART_CUTS)),
        ],
        compiler_params=pltpu.CompilerParams(
            collective_id=0, has_side_effects=True, vmem_limit_bytes=60 * 1024 * 1024
        ),
        name="back_transform",
    )(columns, vectors, factors, order, blocks)
    keep = jnp.arange(slots)[None, :] < live[0][:, None]
    return jnp.where(keep[None, :, :, None], returned, jnp.float32(0.0))


def solution(mesh):
    groups, ring = mesh.shape["group"], mesh.shape["section"] // 2
    placed = (
        P("group", None, None, "section"),
        P("group", None, None, "section"),
        P("group", None, None, None),
        P("group"),
        P("group"),
        P("group", None),
    )
    return jax.shard_map(
        functools.partial(shards, groups, ring),
        mesh=mesh,
        in_specs=placed,
        out_specs=P("group", None, None, "section"),
        check_vma=False,
    )
```

```python
import functools

import jax
import jax.numpy as jnp
from jax import lax
from jax.experimental import pallas as pl
from jax.experimental.pallas import tpu as pltpu
from jax.sharding import PartitionSpec as P

MESH = pl.DeviceIdType.MESH
F32 = jnp.float32
BF16 = jnp.bfloat16
STREAMS = 2
GRAM_CUTS = 4
PART_CUTS = 2


def halves(x):
    first = x.astype(BF16)
    return first, (x - first.astype(F32)).astype(BF16)


def times(a, b):
    return jnp.dot(a, b, preferred_element_type=F32)


def product(a, b):
    return times(a[1], b[0]) + times(a[0], b[1]) + times(a[0], b[0])


def against(a, b):
    return lax.dot_general(a, b, (((1,), (1,)), ((), ())), preferred_element_type=F32)


def tree(ring, skip):
    long = ring // 2
    up = {k: k - 1 for k in range(1, long + 1)}
    up.update({-k: 1 - k for k in range(1, ring - long)})
    if skip and long == 4:
        up[3] = 1
    levels, left = [], set(up)
    while left:
        now = [k for k in left if not any(up[c] == k for c in left)]
        levels.append(sorted(now, key=lambda k: -abs(k)))
        left -= set(now)
    return levels, up


class Place:
    def __init__(self, ring):
        self.ring = ring
        up = tree(ring, True)[1]
        strides = {k - up[k] for k in up} | {1}
        self.near = sorted(strides | {-stride for stride in strides})
        self.group = lax.axis_index("group")
        self.section = lax.axis_index("section")
        self.z = self.section // 2
        self.core = lax.rem(self.section, 2)
        self.way = 1 - 2 * self.core

    def at(self, steps):
        return lax.rem(self.z + self.way * steps + 2 * self.ring, self.ring)

    def neighbour(self, steps):
        return (self.group, self.at(steps) * 2 + self.core)

    def partner(self):
        return (self.group, self.z * 2 + 1 - self.core)


class Sum:
    def __init__(self, place, skip, cuts, src, swapped, landed, full, sent, swap_sem, ring_sem, gather_sem):
        self.p, self.cuts = place, cuts
        self.levels, self.up = tree(place.ring, skip)
        self.edges = sorted(self.up)
        self.src, self.swapped, self.landed, self.full = src, swapped, landed, full
        self.sent, self.swap_sem, self.ring_sem, self.gather_sem = sent, swap_sem, ring_sem, gather_sem
        self.rows = landed.shape[1]
        self.part = self.rows // cuts

    def piece(self, ref, z, core, cut=None):
        start = pl.multiple_of((z * 2 + core) * self.rows, self.part)
        if cut is None:
            return ref.at[pl.ds(start, self.rows)]
        return ref.at[pl.ds(pl.multiple_of(start + cut * self.part, self.part), self.part)]

    def some(self, ref, at, cut):
        return ref.at[at, pl.ds(cut * self.part, self.part)]

    def send(self, src, dst, which, recv, device):
        return pltpu.make_async_remote_copy(
            src_ref=src,
            dst_ref=dst,
            send_sem=self.sent.at[which],
            recv_sem=recv,
            device_id=device,
            device_id_type=MESH,
        )

    def arrived(self, dst, recv):
        self.send(dst, dst, 0, recv, self.p.partner()).wait_recv()

    def swap(self):
        p = self.p
        for k in [k for level in self.levels for k in level] + [0]:
            z = p.at(-k)
            self.send(
                self.piece(self.src, z, 1 - p.core), self.swapped.at[z], 0, self.swap_sem.at[0, z], p.partner()
            ).start()

    def own(self, z, cut):
        return self.piece(self.src, z, self.p.core, cut)[...] + self.some(self.swapped, z, cut)[...]

    def gain(self, k, z, cut):
        value = self.own(z, cut)
        for e, below in enumerate(self.edges):
            if self.up[below] == k:
                part = self.some(self.landed, e, cut)
                self.arrived(part, self.ring_sem.at[e, cut])
                value = value + part[...]
        return value

    def step(self, level):
        p = self.p
        for k in self.levels[level]:
            z = p.at(k)
            self.arrived(self.swapped.at[z], self.swap_sem.at[0, z])
        for cut in range(self.cuts):
            for k in self.levels[level]:
                z, e = p.at(k), self.edges.index(k)
                source = self.some(self.swapped, z, cut)
                source[...] = self.gain(k, z, cut)
                self.send(
                    source, self.some(self.landed, e, cut), 0, self.ring_sem.at[e, cut], p.neighbour(k - self.up[k])
                ).start()

    def total(self, cut):
        p = self.p
        if cut == 0:
            self.arrived(self.swapped.at[p.z], self.swap_sem.at[0, p.z])
        return self.gain(0, p.z, cut)

    def forward(self, k, cut):
        p = self.p
        origin = p.at(-k)
        part = self.piece(self.full, origin, p.core, cut)
        if k:
            self.arrived(part, self.gather_sem.at[self.edges.index(k), cut])
        for e, beyond in sorted(enumerate(self.edges), key=lambda pair: -abs(pair[1])):
            if self.up[beyond] == k:
                self.send(part, part, 1, self.gather_sem.at[e, cut], p.neighbour(beyond - k)).start()
        self.send(part, part, 1, self.swap_sem.at[1, origin], p.partner()).start()

    def spread(self, value, cut):
        p = self.p
        self.piece(self.full, p.z, p.core, cut)[...] = value
        self.forward(0, cut)

    def relay(self, level):
        for cut in range(self.cuts):
            for k in self.levels[len(self.levels) - level]:
                self.forward(k, cut)

    def gathered(self):
        p = self.p
        for z in range(p.ring):
            self.arrived(self.piece(self.full, z, 1 - p.core), self.swap_sem.at[1, z])

    def drain(self):
        pieces = 2 * self.p.ring - 1
        whole = self.full.at[pl.ds(0, pieces * self.rows)]
        for which in range(2):
            self.send(whole, whole, which, self.swap_sem.at[0, 0], self.p.partner()).wait_send()


def kernel(
    groups,
    ring,
    columns,
    vectors,
    factors,
    order,
    blocks,
    out,
    raw,
    facts,
    basis,
    panel,
    moved,
    g_src,
    g_swapped,
    g_landed,
    g_full,
    turned,
    scaled,
    w_src,
    w_swapped,
    w_landed,
    w_full,
    load_sem,
    in_send,
    in_recv,
    out_send,
    out_recv,
    sent,
    swap_sem,
    gram_ring,
    gram_gather,
    ring_sem,
    gather_sem,
):
    p = Place(ring)
    me, section = p.group, p.section
    count, width, rows = raw.shape
    slots = panel.shape[1] // groups

    barrier = pltpu.get_barrier_semaphore()

    def greet(d, carry):
        peer = lax.rem(me + d, groups)
        pl.semaphore_signal(barrier, inc=1, device_id=(peer, section), device_id_type=MESH)
        return carry

    lax.fori_loop(1, groups, greet, 0)
    for other in [p.neighbour(stride) for stride in p.near] + [p.partner()]:
        pl.semaphore_signal(barrier, inc=1, device_id=other, device_id_type=MESH)

    loads = [
        pltpu.make_async_copy(vectors.at[0], raw, load_sem.at[0]),
        pltpu.make_async_copy(factors.at[0], facts, load_sem.at[1]),
    ]
    for s in range(STREAMS):
        loads.append(
            pltpu.make_async_copy(
                columns.at[0, me, pl.ds(s * slots, slots)],
                panel.at[s, pl.ds(pl.multiple_of(me * slots, slots), slots)],
                load_sem.at[2 + s],
            )
        )
    for load in loads:
        load.start()
    loads[0].wait()
    row = section * rows + lax.broadcasted_iota(jnp.int32, (width, rows), 1)
    inside = row < order[0]
    for j in range(count):
        block = jnp.where(inside, raw[j].astype(F32), 0.0)
        basis[pl.ds(j * width, width)] = block.astype(BF16)

    def exchange(s, source, target, send_sem, recv_sem):
        def one(k, carry):
            half = (k + 1) // 2
            d = groups // 2 + (2 * lax.rem(k, 2) - 1) * half
            peer = lax.rem(me + d, groups)
            pltpu.make_async_remote_copy(
                src_ref=source(peer),
                dst_ref=target(me),
                send_sem=send_sem,
                recv_sem=recv_sem,
                device_id=(peer, section),
                device_id_type=MESH,
            ).start()
            return carry

        lax.fori_loop(0, groups - 1, one, 0)

    def lines(ref, s):
        return lambda g: ref.at[s, pl.ds(pl.multiple_of(g * slots, slots), slots)]

    def slab(ref, s):
        return lambda g: ref.at[0, g, pl.ds(s * slots, slots)]

    place_of = {}
    for k in range(1, count):
        low = against(basis[pl.ds(k * width, width)], basis[pl.ds(0, k * width)])
        for j in range(k):
            place_of[k, j] = len(place_of)
            g_src[pl.ds(place_of[k, j] * width, width)] = low[:, j * width : (j + 1) * width]

    gram = Sum(
        p, False, GRAM_CUTS, g_src, g_swapped, g_landed, g_full, sent.at[0], swap_sem.at[0], gram_ring, gram_gather
    )
    parts = [
        Sum(
            p,
            True,
            PART_CUTS,
            w_src.at[s],
            w_swapped.at[s],
            w_landed.at[s],
            w_full.at[s],
            sent.at[1 + s],
            swap_sem.at[1 + s],
            ring_sem.at[s],
            gather_sem.at[s],
        )
        for s in range(STREAMS)
    ]
    pl.semaphore_wait(barrier, groups + len(p.near))
    gram.swap()
    exchange(0, slab(columns, 0), lines(panel, 0), in_send.at[0], in_recv.at[0])
    gram.step(0)
    loads[1].wait()
    for j in range(count):
        factor = jnp.where(j < blocks[0], facts[j], 0.0)
        turned[j] = factor.T
    gram.step(1)
    gram.step(2)
    gram.step(3)
    def substitute(j):
        here, before = pl.ds(j * width, width), pl.ds(0, j * width)
        value = basis[here].astype(F32)
        if j:
            crossed = [g_full[pl.ds(place_of[j, i] * width, width)] for i in range(j)]
            crossed = halves(jnp.concatenate(crossed, axis=1))
            value = value - product(crossed, (scaled[0, before], scaled[1, before]))
        for i, part in enumerate(halves(product(halves(turned[j]), halves(value)))):
            scaled[i, here] = part

    def peer_lines(s):
        whole = panel.at[s, pl.ds(0, (groups - 1) * slots)]
        return whole

    def bring(s):
        loads[2 + s].wait()
        whole = peer_lines(s)
        pltpu.make_async_remote_copy(
            whole, whole, in_send.at[s], in_recv.at[s], device_id=p.partner(), device_id_type=MESH
        ).wait_recv()
        a, b = halves(panel[s])
        v = basis[...]
        w_src[s] = against(b, v) + against(a, v)

    def leave(s):
        moved[s] = panel[s] - product(halves(w_full[s]), (scaled[0], scaled[1]))
        exchange(s, lines(moved, s), slab(out, s), out_send.at[s], out_recv.at[s])
        own = pltpu.make_async_copy(lines(moved, s)(me), slab(out, s)(me), load_sem.at[2 + s])
        own.start()
        return own

    def finish(s):
        for cut in range(PART_CUTS):
            parts[s].spread(parts[s].total(cut), cut)

    for s in range(1, STREAMS):
        exchange(s, slab(columns, s), lines(panel, s), in_send.at[s], in_recv.at[s])
    bring(0)
    parts[0].swap()
    for cut in range(GRAM_CUTS):
        gram.spread(gram.total(cut), cut)
    parts[0].step(0)
    gram.relay(1)
    parts[0].step(1)
    gram.relay(2)
    parts[0].step(2)
    bring(1)
    parts[1].swap()
    gram.relay(3)
    finish(0)
    parts[1].step(0)
    gram.relay(4)
    gram.gathered()
    for j in range(0, 3):
        substitute(j)
    parts[0].relay(1)
    parts[1].step(1)
    for j in range(3, 6):
        substitute(j)
    parts[0].relay(2)
    parts[1].step(2)
    for j in range(6, count):
        substitute(j)
    parts[0].relay(3)
    finish(1)
    parts[0].gathered()
    own0 = leave(0)
    parts[1].relay(1)
    parts[1].relay(2)
    parts[1].relay(3)
    parts[1].gathered()
    own1 = leave(1)

    gram.drain()
    for s in range(STREAMS):
        parts[s].drain()
    own0.wait()
    own1.wait()
    for s in range(STREAMS):
        whole = peer_lines(s)
        pltpu.make_async_remote_copy(
            whole, whole, in_send.at[s], in_recv.at[s], device_id=p.partner(), device_id_type=MESH
        ).wait_send()
        there = pltpu.make_async_remote_copy(
            whole, whole, out_send.at[s], out_recv.at[s], device_id=p.partner(), device_id_type=MESH
        )
        there.wait_send()
        there.wait_recv()


def shards(groups, ring, columns, vectors, factors, order, blocks, live):
    _, count, width, rows = vectors.shape
    slots = columns.shape[2]
    each = slots // STREAMS
    lines = groups * each
    merged = count * width
    gram = count * (count - 1) // 2 * width
    g_piece, w_piece = gram // (2 * ring), lines // (2 * ring)
    anywhere = pl.BlockSpec(memory_space=pl.ANY)
    scalars = pl.BlockSpec(memory_space=pltpu.SMEM)
    returned = pl.pallas_call(
        functools.partial(kernel, groups, ring),
        out_shape=jax.ShapeDtypeStruct(columns.shape, F32),
        in_specs=[anywhere, anywhere, anywhere, scalars, scalars],
        out_specs=anywhere,
        scratch_shapes=[
            pltpu.VMEM((count, width, rows), BF16),
            pltpu.VMEM((count, width, width), F32),
            pltpu.VMEM((merged, rows), BF16),
            pltpu.VMEM((STREAMS, lines, rows), F32),
            pltpu.VMEM((STREAMS, lines, rows), F32),
            pltpu.VMEM((gram, width), F32),
            pltpu.VMEM((ring, g_piece, width), F32),
            pltpu.VMEM((ring - 1, g_piece, width), F32),
            pltpu.VMEM((gram, width), F32),
            pltpu.VMEM((count, width, width), F32),
            pltpu.VMEM((2, merged, rows), BF16),
            pltpu.VMEM((STREAMS, lines, merged), F32),
            pltpu.VMEM((STREAMS, ring, w_piece, merged), F32),
            pltpu.VMEM((STREAMS, ring - 1, w_piece, merged), F32),
            pltpu.VMEM((STREAMS, lines, merged), F32),
            pltpu.SemaphoreType.DMA((2 + STREAMS,)),
            pltpu.SemaphoreType.DMA((STREAMS,)),
            pltpu.SemaphoreType.DMA((STREAMS,)),
            pltpu.SemaphoreType.DMA((STREAMS,)),
            pltpu.SemaphoreType.DMA((STREAMS,)),
            pltpu.SemaphoreType.DMA((1 + STREAMS, 2)),
            pltpu.SemaphoreType.DMA((1 + STREAMS, 2, ring)),
            pltpu.SemaphoreType.DMA((ring - 1, GRAM_CUTS)),
            pltpu.SemaphoreType.DMA((ring - 1, GRAM_CUTS)),
            pltpu.SemaphoreType.DMA((STREAMS, ring - 1, PART_CUTS)),
            pltpu.SemaphoreType.DMA((STREAMS, ring - 1, PART_CUTS)),
        ],
        compiler_params=pltpu.CompilerParams(
            collective_id=0, has_side_effects=True, vmem_limit_bytes=60 * 1024 * 1024
        ),
        name="back_transform",
    )(columns, vectors, factors, order, blocks)
    keep = jnp.arange(slots)[None, :] < live[0][:, None]
    return jnp.where(keep[None, :, :, None], returned, jnp.float32(0.0))


def solution(mesh):
    groups, ring = mesh.shape["group"], mesh.shape["section"] // 2
    placed = (
        P("group", None, None, "section"),
        P("group", None, None, "section"),
        P("group", None, None, None),
        P("group"),
        P("group"),
        P("group", None),
    )
    return jax.shard_map(
        functools.partial(shards, groups, ring),
        mesh=mesh,
        in_specs=placed,
        out_specs=P("group", None, None, "section"),
        check_vma=False,
    )
```
